32 devices in a mesh: cg: 8 (over z, x), vg: 4 (over y, core).
Axes of the slice: x: 2, y: 2, z: 4, core: 2. Of those that a mesh axis runs over, the one named last changes fastest.
Arguments:
- con_embed: float32 [32768, 128], P(('cg', 'vg')), may hold values from -6 to 6
- var_embed: float32 [32768, 128], P(('vg', 'cg')), may hold values from -6 to 6
- row_coef: float32 [32768], P(('cg', 'vg')), may hold values from 0.3 to 3
- col_coef: float32 [32768], P(('vg', 'cg')), may hold values from 0.3 to 3
- self_weight: float32 [128, 128], replicated, may hold values from -0.5 to 0.5
- msg_weight: float32 [128, 128], replicated, may hold values from -0.0234375 to 0.0234375
- timestep: int32 [1], replicated, may hold values from 0 to 999
- tile_rows: int32 [8, 4, 16], P('cg', 'vg'), may hold values from 0 to 7, as said below
- tile_cols: int32 [8, 4, 16], P('cg', 'vg'), may hold values from 0 to 15, as said below
- pattern: bfloat16 [8, 4, 16, 512, 512], P('cg', 'vg'), may hold values from -6 to 6
- cotangent: float32 [32768, 128], P(('cg', 'vg')), may hold values from -6 to 6
Outputs:
- con_update: float32 [32768, 128], P(('cg', 'vg'))
- grad_con: float32 [32768, 128], P(('cg', 'vg'))
- grad_var: float32 [32768, 128], P(('vg', 'cg'))
- grad_msg: float32 [128, 128], replicated
- grad_self: float32 [128, 128], replicated
The draws below stay inside these ranges and needn't reach their ends.
Inputs may be any that keep to these rules, and one draw needn't show every extreme that they name: `tile_rows`: every device lists tile row 0 and tile row 7; a device lists distinct tiles unless 16 exceeds 8 * 16, and repeated tiles add. `tile_cols`: every device lists tile column 0 and tile column 15, together with the rows above: tiles (0, 0) and (7, 15) are on every list.
All inputs are finite; a program needn't handle non-finite values.
Results may differ from the reference program's by a relative error of at most 0.007.
Values may be sent and summed in bfloat16 or wider, within the bound.
A program may use at most 128 MiB of HBM per device.

```python
import math
import jax
import jax.numpy as jnp
from jax import lax

H = 128
TB = 512
C_DEV = 1024
V_DEV = 1024
TILES = 16
NC = 32768
NV = 32768
RBLK = 8
CBLK = 16
N_CG = 8
N_VG = 4


def tile_pairs(key):
    block_total = RBLK * CBLK

    def single(subkey):
        perm_key, roll_key = jax.random.split(subkey)
        middle = jax.random.permutation(perm_key, block_total - 2) + 1
        listing = jnp.concatenate([jnp.array([block_total - 1, 0], dtype=jnp.int32), middle.astype(jnp.int32)])
        chosen = listing[jnp.arange(TILES, dtype=jnp.int32) % block_total]
        offset = jax.random.randint(roll_key, (), 0, TILES)
        return jnp.roll(chosen, offset)
    subkeys = jax.random.split(jax.random.fold_in(key, 11), N_CG * N_VG)
    chosen = jax.vmap(single)(subkeys).reshape(N_CG, N_VG, TILES)
    return (chosen // CBLK, chosen % CBLK)


def draw_tile_rows(key, part):
    return tile_pairs(key)[0]


def draw_tile_cols(key, part):
    return tile_pairs(key)[1]


def steps_of(stream_key, shape, pieces, low, high):
    def one(axis_at, blocks):
        heights = jax.random.uniform(jax.random.fold_in(jax.random.fold_in(stream_key, 6), axis_at), (blocks,), jnp.float32, low / len(pieces), high / len(pieces))
        return jnp.repeat(jnp.exp(heights), shape[axis_at] // blocks).reshape((-1,) + (1,) * (len(shape) - axis_at - 1))

    level = one(*pieces[0])
    for cut in pieces[1:]:
        level = level * one(*cut)
    return level


def gaussian(key, dims, width, most, cuts=(), kind=jnp.bfloat16):
    values = jax.random.normal(key, dims, jnp.float32) * width
    if len(cuts) > 0:
        values = steps_of(key, dims, cuts, -0.22, 0.18) * values
    return jnp.clip(values, min=-most, max=most).astype(kind)


def setup_inputs(seed: int = 0) -> dict:
    key_of = jax.random.split(jax.random.key(seed), 12)
    con_embed = gaussian(key_of[0], (NC, H), 1.0, 6.0, ((0, 32),), jnp.float32)
    var_embed = gaussian(key_of[1], (NV, H), 1.0, 6.0, ((0, 32),), jnp.float32)
    row_coef = jnp.clip(jnp.exp(math.log(3.0) - 2.3025851 * jax.random.uniform(key_of[2], (NC,), jnp.float32) ** steps_of(key_of[2], (NC,), ((0, 32),), -0.2, 0.2)), 0.3, 3.0)
    col_coef = jnp.clip(jnp.exp(math.log(3.0) - 2.3025851 * jax.random.uniform(key_of[3], (NV,), jnp.float32) ** steps_of(key_of[3], (NV,), ((0, 32),), -0.2, 0.2)), 0.3, 3.0)
    self_weight = gaussian(key_of[4], (H, H), H ** -0.5, 0.5, (), jnp.float32)
    msg_weight = gaussian(key_of[5], (H, H), (H * TB) ** -0.5, 0.0234375, (), jnp.float32)
    timestep = jax.random.randint(key_of[6], (1,), 0, 1000).astype(jnp.int32)
    tile_rows = draw_tile_rows(jax.random.fold_in(key_of[11], 71), 0)
    tile_cols = draw_tile_cols(jax.random.fold_in(key_of[11], 71), 0)
    pattern = gaussian(key_of[9], (N_CG, N_VG, TILES, TB, TB), 1.0, 6.0, ((0, 8), (1, 4)))
    cotangent = gaussian(key_of[10], (NC, H), 1.0, 6.0, ((0, 32),), jnp.float32)
    return dict(con_embed=con_embed, var_embed=var_embed, row_coef=row_coef, col_coef=col_coef, self_weight=self_weight, msg_weight=msg_weight, timestep=timestep, tile_rows=tile_rows, tile_cols=tile_cols, pattern=pattern, cotangent=cotangent)


def reference(con_embed, var_embed, row_coef, col_coef, self_weight, msg_weight, timestep, tile_rows, tile_cols, pattern, cotangent):
    highest = lax.Precision.HIGHEST
    group_rows = C_DEV * N_VG
    group_cols = V_DEV * N_CG
    row_list = tile_rows.reshape(-1, TILES)
    col_list = tile_cols.reshape(-1, TILES)
    pattern_list = pattern.reshape(-1, TILES, TB, TB)
    devices = jnp.arange(N_CG * N_VG, dtype=jnp.int32)
    projected = (jnp.dot(var_embed, msg_weight, precision=highest, preferred_element_type=jnp.float32) * col_coef[:, None]).astype(jnp.bfloat16)

    def forward(running, device):
        con_group = device // N_VG
        var_group = device % N_VG
        source = lax.dynamic_slice_in_dim(projected, (var_group * group_cols).astype(jnp.int32), group_cols, 0)
        source = source.reshape(CBLK, TB, H).astype(jnp.float32)
        tile_mask = pattern_list[device].astype(jnp.float32)
        products = jnp.einsum('trc,tch->trh', tile_mask, source[col_list[device]], precision=highest)
        selector = (row_list[device][None, :] == jnp.arange(RBLK, dtype=jnp.int32)[:, None]).astype(jnp.float32)
        partial_value = jnp.einsum('bt,trh->brh', selector, products, precision=highest).reshape(group_rows, H)
        offset = (con_group * group_rows).astype(jnp.int32)
        current = lax.dynamic_slice_in_dim(running, offset, group_rows, 0)
        return lax.dynamic_update_slice_in_dim(running, current + partial_value, offset, 0), None

    messages, _ = lax.scan(forward, jnp.zeros((NC, H), jnp.float32), devices)
    frequency = jnp.exp(-math.log(10000.0) * jnp.arange(H // 2, dtype=jnp.float32) / (H // 2))
    phases = timestep[0].astype(jnp.float32) * frequency
    time_embed = jnp.concatenate([jnp.sin(phases), jnp.cos(phases)])
    preact = jnp.dot(con_embed, self_weight, precision=highest, preferred_element_type=jnp.float32) + row_coef[:, None] * messages + time_embed[None, :]
    sigmoid_z = jax.nn.sigmoid(preact)
    con_update = con_embed + preact * sigmoid_z
    grad_pre = cotangent * sigmoid_z * (1.0 + preact * (1.0 - sigmoid_z))
    grad_con = cotangent + jnp.dot(grad_pre, self_weight.T, precision=highest, preferred_element_type=jnp.float32)
    grad_self = jnp.dot(con_embed.T, grad_pre, precision=highest, preferred_element_type=jnp.float32)
    grad_messages = (row_coef[:, None] * grad_pre).astype(jnp.bfloat16)

    def backward(running, device):
        con_group = device // N_VG
        var_group = device % N_VG
        source = lax.dynamic_slice_in_dim(grad_messages, (con_group * group_rows).astype(jnp.int32), group_rows, 0)
        source = source.reshape(RBLK, TB, H).astype(jnp.float32)
        tile_mask = pattern_list[device].astype(jnp.float32)
        products = jnp.einsum('trc,trh->tch', tile_mask, source[row_list[device]], precision=highest)
        selector = (col_list[device][None, :] == jnp.arange(CBLK, dtype=jnp.int32)[:, None]).astype(jnp.float32)
        partial_value = jnp.einsum('bt,tch->bch', selector, products, precision=highest).reshape(group_cols, H)
        offset = (var_group * group_cols).astype(jnp.int32)
        current = lax.dynamic_slice_in_dim(running, offset, group_cols, 0)
        return lax.dynamic_update_slice_in_dim(running, current + partial_value, offset, 0), None

    grad_projected, _ = lax.scan(backward, jnp.zeros((NV, H), jnp.float32), devices)
    grad_lin = col_coef[:, None] * grad_projected
    grad_var = jnp.dot(grad_lin, msg_weight.T, precision=highest, preferred_element_type=jnp.float32)
    grad_msg = jnp.dot(var_embed.T, grad_lin, precision=highest, preferred_element_type=jnp.float32)
    return (con_update, grad_con, grad_var, grad_msg, grad_self)
```

```python
import functools
import math

import jax
import jax.numpy as jnp
import numpy as np
from jax import lax
from jax.experimental import pallas as pl
from jax.experimental.pallas import tpu as pltpu
from jax.sharding import PartitionSpec as P

H = 128
TB = 512
CHUNKS = 4
MESH = pl.DeviceIdType.MESH
HIGHEST = lax.Precision.HIGHEST
F32 = jnp.float32
BF16 = jnp.bfloat16


def rcopy(src, dst, send_sem, recv_sem, device):
    return pltpu.make_async_remote_copy(
        src_ref=src, dst_ref=dst, send_sem=send_sem, recv_sem=recv_sem,
        device_id=device, device_id_type=MESH,
    )


def rows(index, size):
    return pl.ds(pl.multiple_of(index * size, size), size)


def dot(a, b, dims=((1,), (0,))):
    return lax.dot_general(a, b, (dims, ((), ())), precision=HIGHEST, preferred_element_type=F32)


def column(coef_ref, out_ref):
    for i in range(coef_ref.shape[0]):
        out_ref[pl.ds(i * H, H), :] = jnp.broadcast_to(coef_ref[pl.ds(i, 1), :], (H, H)).T


class Total:
    def __init__(self, n_cg, n_vg, local, out, cuts, parts, sem):
        self.n_cg, self.n_vg = n_cg, n_vg
        self.local, self.out, self.cuts, self.parts, self.sem = local, out, cuts, parts, sem
        self.cg, self.vg = lax.axis_index("cg"), lax.axis_index("vg")
        self.size = H // n_cg

    def a(self, j):
        c = lax.rem(self.cg + j, self.n_cg)
        return rcopy(
            self.local.at[:, rows(c, self.size), :], self.cuts.at[j - 1],
            self.sem.at[0, j], self.sem.at[1, j], (c, self.vg),
        )

    def b(self, j):
        v = lax.rem(self.vg + j, self.n_vg)
        block = self.parts.at[self.vg]
        return rcopy(block, block, self.sem.at[2, j], self.sem.at[3, j], (self.cg, v))

    def b_wait(self, j):
        v = lax.rem(self.vg + self.n_vg - j, self.n_vg)
        block = self.parts.at[v]
        rcopy(block, block, self.sem.at[2, j], self.sem.at[3, j], (self.cg, v)).wait_recv()

    def c(self, j):
        c = lax.rem(self.cg + j, self.n_cg)
        block = self.out.at[:, rows(self.cg, self.size), :]
        return rcopy(block, block, self.sem.at[4, j], self.sem.at[5, j], (c, self.vg))

    def c_wait(self, j):
        c = lax.rem(self.cg + self.n_cg - j, self.n_cg)
        block = self.out.at[:, rows(c, self.size), :]
        rcopy(block, block, self.sem.at[4, j], self.sem.at[5, j], (c, self.vg)).wait_recv()

    def start(self):
        for j in range(1, self.n_cg):
            self.a(j).start()

    def second(self):
        value = self.local[:, rows(self.cg, self.size), :]
        for j in range(1, self.n_cg):
            self.a(j).wait_recv()
            value = value + self.cuts[j - 1]
        self.parts[self.vg] = value
        for j in range(1, self.n_vg):
            self.b(j).start()

    def third(self):
        for j in range(1, self.n_vg):
            self.b_wait(j)
        value = self.parts[0]
        for v in range(1, self.n_vg):
            value = value + self.parts[v]
        self.out[:, rows(self.cg, self.size), :] = value
        for j in range(1, self.n_cg):
            self.c(j).start()

    def finish(self):
        for j in range(1, self.n_cg):
            self.c_wait(j)
            self.c(j).wait_send()
            self.a(j).wait_send()
        for j in range(1, self.n_vg):
            self.b(j).wait_send()


def chains(count, row_blocks, col_blocks, row_ref, col_ref, out_ref):
    base = 0
    for index_ref, blocks in ((row_ref, row_blocks), (col_ref, col_blocks)):
        index = [index_ref[k] for k in range(count)]
        for k in range(count):
            at = jnp.int32(count)
            for j in range(k):
                at = jnp.where(index[j] == index[k], j, at)
            out_ref[base + k] = at

        def last(b, carry):
            at = jnp.int32(count)
            for k in range(count):
                at = jnp.where(index[k] == b, k, at)
            out_ref[base + count + b] = at
            return carry

        lax.fori_loop(0, blocks, last, 0)
        base = base + count + blocks


def layer_kernel(
    n_cg, n_vg, row_ref, col_ref, step_ref, pattern_hbm, var_ref, msg_w_ref, col_coef_ref, con_hbm, cot_hbm,
    self_w_ref, row_coef_ref, freq_ref,
    update_ref, grad_con_ref, grad_var_ref, grad_msg_ref, grad_self_ref,
    pattern, con_ref, cot_ref, col_scale, row_scale, pre, sums, grads, projected_a, projected_b, whole_a, whole_b, acc, chain_ref,
    to_core, from_core, to_peer, from_peer, to_x, from_x, to_z, from_z, to_q, from_q,
    local, total, cuts, parts,
    load_sem, gz_send, gx_send, gz_recv, gx_recv, gq_send, gq_recv,
    core_send, core_recv, peer_send, peer_recv, own_send, pass_send, block_recv, pair_recv,
    x_send, x_recv, z_send, z_recv, q_send, q_recv, total_sem,
):
    n_z, n_hi = n_cg // 2, n_vg // 2
    cg, vg = lax.axis_index("cg"), lax.axis_index("vg")
    z, x = cg // 2, cg % 2
    hi, core = vg // 2, vg % 2
    count = pattern.shape[0]
    size = var_ref.shape[0]
    piece = size // CHUNKS
    tiles = size // TB
    halves = CHUNKS // tiles
    half = TB // halves
    chunks = range(CHUNKS)
    early, late = range(tiles), range(CHUNKS - tiles, CHUNKS)
    projected, whole = (projected_a, projected_b), (whole_a, whole_b)
    odd = z % 2
    mate = z + 1 - 2 * odd
    x_peer, z_mate, pair = (z * 2 + 1 - x, vg), (mate * 2 + x, vg), (cg, hi * 2 + 1 - core)

    barrier = pltpu.get_barrier_semaphore()
    for j in range(1, n_cg):
        pl.semaphore_signal(barrier, inc=1, device_id=(lax.rem(cg + j, n_cg), vg), device_id_type=MESH)
    for j in range(1, n_vg):
        pl.semaphore_signal(barrier, inc=1, device_id=(cg, lax.rem(vg + j, n_vg)), device_id_type=MESH)
    loads = [
        pltpu.make_async_copy(con_hbm, con_ref, load_sem.at[0]),
        pltpu.make_async_copy(cot_hbm, cot_ref, load_sem.at[1]),
        pltpu.make_async_copy(pattern_hbm, pattern, load_sem.at[2]),
    ]
    for load in loads:
        load.start()

    def of(h):
        return range(h * tiles, (h + 1) * tiles)

    def cut(block, k):
        return rows(block * CHUNKS + k, piece)

    def here(k):
        return pl.ds((k % tiles) * TB + (k // tiles) * half, half)

    def inner(k):
        return pl.ds((k // tiles) * half, half)

    def spot(parts_of, block, k):
        return parts_of[k // tiles].at[block * tiles + k % tiles]

    def gz_copy(zs, way, k):
        block = spot(projected, zs * 2 + x, k)
        step = 1 if way == 0 else -1
        return rcopy(block, block, gz_send.at[way, zs, k], gz_recv.at[zs, k], ((z + step) * 2 + x, vg))

    def gx_copy(zs, k):
        block = spot(projected, zs * 2 + x, k)
        return rcopy(block, block, gx_send.at[zs, k], gx_recv.at[zs, k], x_peer)

    def gx_wait(zs, k):
        block = spot(projected, zs * 2 + 1 - x, k)
        rcopy(block, block, gx_send.at[zs, k], gx_recv.at[zs, k], x_peer).wait_recv()

    def gq_copy(k):
        block = spot(projected, z * 2 + 1 - x, k)
        return rcopy(block, block, gq_send.at[k - late[0]], gq_recv.at[k - late[0]], z_mate)

    def gq_wait(k):
        block = spot(projected, mate * 2 + 1 - x, k)
        rcopy(block, block, gq_send.at[k - late[0]], gq_recv.at[k - late[0]], z_mate).wait_recv()

    def on(zs, way, act):
        if way == 0:
            pl.when((zs >= 0) & (zs <= z) & (z + 1 < n_z))(act)
        else:
            pl.when((zs < n_z) & (zs >= z) & (z >= 1))(act)

    def by_x(d, way, k):
        if d != 1 or k not in late:
            return None
        return odd == 0 if way == 0 else odd == 1

    def by_x_back(zd, k):
        return zd != mate if k in early else None

    def when(condition, act):
        if condition is None:
            act()
        else:
            pl.when(condition)(act)

    column(col_coef_ref, col_scale)
    for k in chunks:
        spot(projected, cg, k)[...] = (var_ref[here(k), :] * col_scale[here(k), :]).astype(BF16)
        if k == 0:
            pl.semaphore_wait(barrier, n_cg + n_vg - 2)
        for way in (0, 1):
            on(z, way, lambda way=way: gz_copy(z, way, k).start())
        gx_copy(z, k).start()

    acc[count] = jnp.zeros(acc.shape[1:], F32)
    row_blocks = whole_a.shape[0]
    chains(count, row_blocks, projected_a.shape[0], row_ref, col_ref, chain_ref)
    last_f, prev_b, last_b = count, count + row_blocks, 2 * count + row_blocks

    for d in range(1, n_z):
        for k in chunks:
            for way in (0, 1):
                zs = z - d if way == 0 else z + d

                @pl.when((zs >= 0) & (zs < n_z))
                def _(zs=zs, way=way, k=k, d=d):
                    gz_copy(zs, way, k).wait_recv()
                    on(zs, way, lambda: gz_copy(zs, way, k).start())
                    when(by_x(d, way, k), lambda: gx_copy(zs, k).start())

        to_go = n_z - 1 - z
        if d == 1:
            turn = ((odd == 0) & (z <= 1)) | ((odd == 1) & (to_go <= 1))
        else:
            turn = ((odd == 0) & (z == d)) | ((odd == 1) & (to_go == d))

        @pl.when(turn)
        def _():
            for k in late:
                gx_wait(z, k)
                gq_copy(k).start()

    for load in loads[:2]:
        load.wait()
    phases = step_ref[0].astype(F32) * freq_ref[...]
    lane = lax.broadcasted_iota(jnp.int32, phases.shape, 1)
    time_embed = jnp.where(lane < H // 2, jnp.sin(phases), jnp.cos(phases))
    pre[...] = dot(con_ref[...], self_w_ref[...]) + time_embed
    column(row_coef_ref, row_scale)
    loads[2].wait()

    def tile_first(from_ref, source_refs, side):
        def step(k, carry):
            source = source_refs[0][from_ref[k]]
            tile = pattern[k, :, pl.ds(0, half)] if side == 1 else pattern[k, pl.ds(0, half), :]
            acc[k] = lax.dot_general(tile, source, (((side,), (0,)), ((), ())), preferred_element_type=F32)
            return carry

        lax.fori_loop(0, count, step, 0, unroll=4)

    def tile_next(prev, from_ref, source_refs, side, h, m):
        deep, span = pl.ds(h * half, half), pl.ds(m * half, half)

        def step(k, carry):
            source = source_refs[h][from_ref[k]]
            tile = pattern[k, span, deep] if side == 1 else pattern[k, deep, span]
            product = lax.dot_general(tile, source, (((side,), (0,)), ((), ())), preferred_element_type=F32)
            value = acc[k, span, :] + product
            if h == halves - 1:
                value = value + acc[chain_ref[prev + k], span, :]
            acc[k, span, :] = value
            return carry

        lax.fori_loop(0, count, step, 0, unroll=4)

    def part(last, block, k):
        tile = chain_ref[last + block * tiles + k % tiles]
        return acc[tile, inner(k), :]

    base = z - odd
    for h in range(halves):
        for k in of(h):
            if k in late:
                gq_wait(k)
                for j in range(2, n_z):
                    gx_wait(lax.rem(base + j, n_z), k)
            else:
                for zs in range(n_z):
                    gx_wait(zs, k)
        if h == 0:
            tile_first(col_ref, projected, 1)
        elif h < halves - 1:
            for m in range(halves):
                tile_next(0, col_ref, projected, 1, h, m)

    ups = [lax.rem(hi + j, n_hi) for j in range(n_hi)]
    downs = [lax.rem(hi + n_hi - j, n_hi) for j in range(n_hi)]

    def core_copy(h, k):
        return rcopy(
            to_core.at[cut(h, k), :], from_core.at[cut(h, k), :], core_send.at[h, k], core_recv.at[h, k], pair
        )

    def peer_copy(j, k):
        return rcopy(
            to_peer.at[cut(j - 1, k), :], from_peer.at[cut(j - 1, k), :],
            peer_send.at[j - 1, k], peer_recv.at[j - 1, k], (cg, ups[j] * 2 + core),
        )

    def own_copy(j, k):
        block = spot(whole, vg, k)
        return rcopy(block, block, own_send.at[j - 1, k], block_recv.at[j - 1, k], (cg, ups[j] * 2 + core))

    def block_wait(j, k):
        block = spot(whole, downs[j] * 2 + core, k)
        rcopy(block, block, own_send.at[j - 1, k], block_recv.at[j - 1, k], pair).wait_recv()

    def pass_copy(h, k):
        block = spot(whole, h * 2 + core, k)
        return rcopy(block, block, pass_send.at[h, k], pair_recv.at[h, k], pair)

    def pass_wait(h, k):
        block = spot(whole, h * 2 + 1 - core, k)
        rcopy(block, block, pass_send.at[h, k], pair_recv.at[h, k], pair).wait_recv()

    for m in range(halves):
        tile_next(0, col_ref, projected, 1, halves - 1, m)
        for j in list(range(1, n_hi)) + [0]:
            for k in of(m):
                to_core[cut(ups[j], k), :] = part(last_f, ups[j] * 2 + 1 - core, k).astype(BF16)
                core_copy(ups[j], k).start()
    for j in range(1, n_hi):
        for k in chunks:
            core_copy(ups[j], k).wait_recv()
            to_peer[cut(j - 1, k), :] = (
                part(last_f, ups[j] * 2 + core, k) + from_core[cut(ups[j], k), :].astype(F32)
            ).astype(BF16)
            peer_copy(j, k).start()
    for k in chunks:
        core_copy(hi, k).wait_recv()
        value = part(last_f, vg, k) + from_core[cut(hi, k), :].astype(F32)
        for j in range(1, n_hi):
            peer_copy(j, k).wait_recv()
            value = value + from_peer[cut(j - 1, k), :].astype(F32)
        sums[here(k), :] = value
        preact = pre[here(k), :] + row_scale[here(k), :] * dot(value, msg_w_ref[...])
        sig = jax.nn.sigmoid(preact)
        grad_pre = cot_ref[here(k), :] * sig * (1.0 + preact * (1.0 - sig))
        grad = row_scale[here(k), :] * grad_pre
        spot(whole, vg, k)[...] = dot(grad, msg_w_ref[...], ((1,), (1,))).astype(BF16)
        for j in range(1, n_hi):
            own_copy(j, k).start()
        pass_copy(hi, k).start()
        grads[here(k), :] = grad
        update_ref[here(k), :] = con_ref[here(k), :] + preact * sig
        pre[here(k), :] = grad_pre
    small = Total(n_cg, n_vg, local, total, cuts, parts, total_sem)

    def take(h):
        for k in of(h):
            for j in range(1, n_hi):
                block_wait(j, k)
                pass_copy(downs[j], k).start()

    take(0)
    local[0] = dot(sums[...], grads[...], ((0,), (0,)))
    local[1] = dot(con_ref[...], pre[...], ((0,), (0,)))
    small.start()
    for h in range(halves):
        if h > 0:
            take(h)
        for k in of(h):
            for hb in range(n_hi):
                pass_wait(hb, k)
        if h == 0:
            tile_first(row_ref, whole, 0)
        elif h < halves - 1:
            for m in range(halves):
                tile_next(prev_b, row_ref, whole, 0, h, m)

    def x_copy(zd, k):
        return rcopy(to_x.at[cut(zd, k), :], from_x.at[cut(zd, k), :], x_send.at[zd, k], x_recv.at[zd, k], x_peer)

    def q_copy(k):
        return rcopy(to_q.at[rows(k, piece), :], from_q.at[rows(k, piece), :], q_send.at[k], q_recv.at[k], z_mate)

    def z_copy(zd, way, k):
        step = 1 if way == 0 else -1
        return rcopy(
            to_z.at[cut(zd, k), :], from_z.at[way, cut(zd, k), :],
            z_send.at[way, zd, k], z_recv.at[way, zd, k], ((z + step) * 2 + x, vg),
        )

    def z_arrives(way):
        return z >= 1 if way == 0 else z + 1 < n_z

    turns = range(n_z - 1)

    def targets(t):
        yield n_z - 1 - t, 0, n_z - 1 - t > z
        yield t, 1, t < z

    def send_x(zd, k):
        to_x[cut(zd, k), :] = part(last_b, zd * 2 + 1 - x, k).astype(BF16)
        x_copy(zd, k).start()

    def send_turn(t, span):
        for zd, way, there in targets(t):

            @pl.when(there)
            def _(zd=zd):
                for k in span:
                    when(by_x_back(zd, k), lambda: send_x(zd, k))

    for m in range(halves):
        tile_next(prev_b, row_ref, whole, 0, halves - 1, m)
        for k in of(m):
            if k in early:
                to_q[rows(k, piece), :] = part(last_b, mate * 2 + 1 - x, k).astype(BF16)
                q_copy(k).start()
        send_turn(0, of(m))
    for t in turns[1:]:
        send_turn(t, chunks)
    grad_con_ref[...] = cot_ref[...] + dot(pre[...], self_w_ref[...], ((1,), (1,)))

    for t in turns:
        for k in chunks:
            for zd, way, there in targets(t):

                @pl.when(there)
                def _(zd=zd, way=way, k=k):
                    sums[here(k), :] = part(last_b, zd * 2 + x, k)

                    def from_peer_x():
                        x_copy(zd, k).wait_recv()
                        sums[here(k), :] += from_x[cut(zd, k), :].astype(F32)

                    when(by_x_back(zd, k), from_peer_x)

                    @pl.when(z_arrives(way))
                    def _():
                        z_copy(zd, way, k).wait_recv()
                        sums[here(k), :] += from_z[way, cut(zd, k), :].astype(F32)

                    to_z[cut(zd, k), :] = sums[here(k), :].astype(BF16)
                    z_copy(zd, way, k).start()

            if t == 0 and k == 1:
                small.second()
        if t == 0:
            small.third()
            for k in chunks:
                if k in early:
                    q_copy(k).wait_recv()
                    to_x[cut(z, k), :] = (
                        part(last_b, z * 2 + 1 - x, k) + from_q[rows(k, piece), :].astype(F32)
                    ).astype(BF16)
                    x_copy(z, k).start()
                else:
                    send_x(z, k)

    for k in chunks:
        x_copy(z, k).wait_recv()
        sums[here(k), :] = part(last_b, cg, k) + from_x[cut(z, k), :].astype(F32)
        for way in (0, 1):
            @pl.when(z_arrives(way))
            def _(way=way, k=k):
                z_copy(z, way, k).wait_recv()
                sums[here(k), :] += from_z[way, cut(z, k), :].astype(F32)

        grad_var_ref[here(k), :] = sums[here(k), :] * col_scale[here(k), :]

    small.finish()
    grad_msg_ref[...] = total[0]
    grad_self_ref[...] = total[1]
    for k in chunks:
        for d in range(n_z):
            for way in (0, 1) if d else (0,):
                zs = z - d if way == 0 else z + d

                @pl.when((zs >= 0) & (zs < n_z))
                def _(zs=zs, d=d, way=way, k=k):
                    when(by_x(d, way, k), lambda: gx_copy(zs, k).wait_send())

        x_copy(z, k).wait_send()
        for d in range(n_z):
            for way in (0, 1):
                zs = z - d if way == 0 else z + d
                on(zs, way, lambda zs=zs, way=way, k=k: gz_copy(zs, way, k).wait_send())
        for t in turns:
            for zd, way, there in targets(t):

                @pl.when(there)
                def _(zd=zd, way=way, k=k):
                    when(by_x_back(zd, k), lambda: x_copy(zd, k).wait_send())
                    z_copy(zd, way, k).wait_send()

        for h in range(n_hi):
            pass_copy(h, k).wait_send()
            core_copy(h, k).wait_send()
        for j in range(1, n_hi):
            peer_copy(j, k).wait_send()
            own_copy(j, k).wait_send()
        if k in late:
            gq_copy(k).wait_send()
        if k in early:
            q_copy(k).wait_send()


def layer(row_index, col_index, timestep, patterns, var_embed, msg_weight, col_coef, con_embed, cotangent,
          self_weight, row_coef, frequency, n_cg, n_vg):
    size = var_embed.shape[0]
    count = patterns.shape[0]
    n_z, n_hi, n_max = n_cg // 2, n_vg // 2, max(n_cg, n_vg)
    others = max(n_hi - 1, 1)
    row_blocks, col_blocks = n_vg * size // TB, n_cg * size // TB
    early = size // TB
    share = H // n_cg
    vmem, smem, anywhere = (pl.BlockSpec(memory_space=m) for m in (pltpu.VMEM, pltpu.SMEM, pl.ANY))
    full, square = pltpu.VMEM((size, H), F32), pltpu.VMEM((H, H), F32)
    dma = lambda *n: pltpu.SemaphoreType.DMA(n)
    return pl.pallas_call(
        functools.partial(layer_kernel, n_cg, n_vg),
        name="layer",
        out_shape=(full, full, full, square, square),
        in_specs=[smem, smem, smem, anywhere, vmem, vmem, vmem, anywhere, anywhere, vmem, vmem, vmem],
        out_specs=(vmem,) * 5,
        scratch_shapes=[
            pltpu.VMEM(patterns.shape, BF16),
            *[pltpu.VMEM((size, H), F32)] * 7,
            *[pltpu.VMEM((col_blocks, TB // 2, H), BF16)] * 2,
            *[pltpu.VMEM((row_blocks, TB // 2, H), BF16)] * 2,
            pltpu.VMEM((count + 1, TB, H), F32),
            pltpu.SMEM((2 * count + row_blocks + col_blocks,), jnp.int32),
            pltpu.VMEM((n_hi * size, H), BF16),
            pltpu.VMEM((n_hi * size, H), BF16),
            pltpu.VMEM((others * size, H), BF16),
            pltpu.VMEM((others * size, H), BF16),
            pltpu.VMEM((n_z * size, H), BF16),
            pltpu.VMEM((n_z * size, H), BF16),
            pltpu.VMEM((n_z * size, H), BF16),
            pltpu.VMEM((2, n_z * size, H), BF16),
            pltpu.VMEM((early * (size // CHUNKS), H), BF16),
            pltpu.VMEM((early * (size // CHUNKS), H), BF16),
            pltpu.VMEM((2, H, H), F32),
            pltpu.VMEM((2, H, H), F32),
            pltpu.VMEM((n_cg - 1, 2, share, H), F32),
            pltpu.VMEM((n_vg, 2, share, H), F32),
            dma(3), dma(2, n_z, CHUNKS), dma(n_z, CHUNKS), dma(n_z, CHUNKS), dma(n_z, CHUNKS),
            dma(early), dma(early),
            dma(n_hi, CHUNKS), dma(n_hi, CHUNKS), dma(others, CHUNKS), dma(others, CHUNKS),
            dma(others, CHUNKS), dma(n_hi, CHUNKS), dma(others, CHUNKS), dma(n_hi, CHUNKS),
            dma(n_z, CHUNKS), dma(n_z, CHUNKS), dma(2, n_z, CHUNKS), dma(2, n_z, CHUNKS),
            dma(early), dma(early), dma(6, n_max),
        ],
        compiler_params=pltpu.CompilerParams(
            collective_id=0, has_side_effects=True, vmem_limit_bytes=60000 * 1024
        ),
    )(
        row_index, col_index, timestep, patterns, var_embed, msg_weight, col_coef.reshape(-1, H),
        con_embed, cotangent, self_weight, row_coef.reshape(-1, H), frequency,
    )


def finish_kernel(*refs):
    count = (len(refs) - 1) // 2
    copies = [pltpu.make_async_copy(refs[i], refs[count + i], refs[-1].at[i]) for i in range(count)]
    for copy in copies:
        copy.start()
    for copy in copies:
        copy.wait()


def finish(*arrays):
    return pl.pallas_call(
        finish_kernel,
        name="finish",
        out_shape=tuple(jax.ShapeDtypeStruct(a.shape, a.dtype) for a in arrays),
        in_specs=[pl.BlockSpec(memory_space=pltpu.VMEM)] * len(arrays),
        out_specs=(pl.BlockSpec(memory_space=pl.ANY),) * len(arrays),
        scratch_shapes=[pltpu.SemaphoreType.DMA((len(arrays),))],
    )(*[pltpu.with_memory_space_constraint(a, pltpu.VMEM) for a in arrays])


def body(
    con_embed, var_embed, row_coef, col_coef, self_weight, msg_weight,
    timestep, tile_rows, tile_cols, pattern, cotangent,
):
    n_cg, n_vg = lax.axis_size("cg"), lax.axis_size("vg")
    frequency = np.exp(-math.log(10000.0) * np.arange(H // 2) / (H // 2))
    frequency = jnp.asarray(np.concatenate([frequency, frequency])[None, :], F32)
    return finish(*layer(
        tile_rows.reshape(-1), tile_cols.reshape(-1), timestep, pattern.reshape(-1, TB, TB), var_embed, msg_weight,
        col_coef, con_embed, cotangent, self_weight, row_coef, frequency, n_cg, n_vg,
    ))


def solution(mesh):
    in_specs = (
        P(("cg", "vg"), None),
        P(("vg", "cg"), None),
        P(("cg", "vg")),
        P(("vg", "cg")),
        P(),
        P(),
        P(),
        P("cg", "vg", None),
        P("cg", "vg", None),
        P("cg", "vg", None, None, None),
        P(("cg", "vg"), None),
    )
    out_specs = (P(("cg", "vg"), None), P(("cg", "vg"), None), P(("vg", "cg"), None), P(), P())
    return jax.shard_map(body, mesh=mesh, in_specs=in_specs, out_specs=out_specs, check_vma=False)
```
